32 devices in a mesh: particle: 4 (over x, core), rows: 8 (over z, y).
Axes of the slice: x: 2, y: 2, z: 4, core: 2. Of those that a mesh axis runs over, the one named last changes fastest.
Arguments:
- latent: bfloat16 [4, 32, 24, 640], P('particle', 'rows'), may hold values from -20 to 20
- ada_scale: float32 [640], replicated, may hold values from -0.5 to 0.5
- ada_shift: float32 [640], replicated, may hold values from -3 to 3
- conv_weight: bfloat16 [5760, 640], P('rows'), may hold values from -0.078125 to 0.078125
- qkv_weight: bfloat16 [640, 1920], replicated, may hold values from -1.4230249 to 1.4230249
- out_weight: bfloat16 [640, 640], replicated, may hold values from -0.25 to 0.25
- ancestors: int32 [4], replicated, may hold values from 0 to 3
Outputs:
- resampled: bfloat16 [4, 32, 24, 640], P('particle', 'rows')
The draws below stay inside these ranges and needn't reach their ends.
All inputs are finite; a program needn't handle non-finite values.
Results may differ from the reference program's by a relative error of at most 0.0081.
Values may be sent and summed in bfloat16 or wider, within the bound.
A program may use at most 64 MiB of HBM per device.

```python
import math
import jax
import jax.numpy as jnp
from jax import lax

C = 640
HEADS = 10
GROUPS = 32
W = 24
H = 32
PARTICLES = 4


def draw_latent(key, part):
    key_z, key_c = jax.random.split(key, 2)
    row_scale = 0.5 * 3.0 ** (jnp.arange(H, dtype=jnp.float32) / max(H - 1, 1))
    chan_scale = jnp.exp(jax.random.uniform(key_c, (C,), jnp.float32, math.log(0.3), math.log(3.0)))
    base = jnp.clip(jax.random.normal(key_z, (PARTICLES, H, W, C), jnp.float32), -4.0, 4.0)
    return (base * row_scale[None, :, None, None] * chan_scale).astype(jnp.bfloat16)


def draw_qkv_weight(key, part):
    base = jnp.clip(jax.random.normal(key, (C, 3 * C), jnp.float32), -6.0, 6.0) / math.sqrt(C)
    return base.astype(jnp.bfloat16)


def place_ends(result, own_key, smallest, largest):
    longest = result.shape.index(max(result.shape))
    spots = []
    for shift in (0, 1):
        where = [jax.random.randint(jax.random.fold_in(own_key, axis), (), 0, length) for axis, length in enumerate(result.shape)]
        where[longest] = (where[longest] + shift) % result.shape[longest]
        spots.append(tuple(where))
    return result.at[spots[0]].set(smallest).at[spots[1]].set(largest)


def steps_of(key, extent, cuts, low, largest):
    level, own = 1.0, jax.random.fold_in(key, 6)
    for dim, blocks in cuts:
        steps = jnp.exp(jax.random.uniform(jax.random.fold_in(own, dim), (blocks,), jnp.float32, low / len(cuts), largest / len(cuts)))
        level = level * jnp.repeat(steps, extent[dim] // blocks).reshape([-1 if axis == dim else 1 for axis in range(len(extent))])
    return level


def noise(rng, shape, deviation, limit, pieces=(), held_as=jnp.bfloat16):
    entries = jax.random.normal(rng, shape, jnp.float32) * deviation
    if len(pieces) > 0:
        entries = steps_of(rng, shape, pieces, -0.22, 0.18) * entries
    return jnp.clip(entries, min=-limit, max=limit).astype(held_as)


def setup_inputs(seed: int = 0) -> dict:
    streams_of = jax.random.split(jax.random.key(seed), 8)
    latent = draw_latent(jax.random.fold_in(streams_of[7], 71), 0)
    ada_scale = jnp.clip(jax.random.uniform(streams_of[1], (C,), jnp.float32, -0.5, 0.5), -0.5, 0.5)
    ada_shift = noise(streams_of[2], (C,), 0.5, 3.0, (), jnp.float32)
    conv_weight = noise(streams_of[3], (9 * C, C), (9 * C) ** -0.5, 0.078125, ((0, 8),))
    qkv_weight = draw_qkv_weight(jax.random.fold_in(streams_of[7], 71), 0)
    out_weight = noise(streams_of[5], (C, C), C ** -0.5, 0.25)
    ancestors = place_ends(jax.random.randint(streams_of[6], (PARTICLES,), 0, PARTICLES), jax.random.fold_in(streams_of[6], 1), 0, PARTICLES - 1).astype(jnp.int32)
    return {"latent": latent, "ada_scale": ada_scale, "ada_shift": ada_shift, "conv_weight": conv_weight, "qkv_weight": qkv_weight, "out_weight": out_weight, "ancestors": ancestors}


def group_norm(values):
    grouped = values.reshape(values.shape[0], GROUPS, -1)
    count = grouped.shape[0] * grouped.shape[2]
    mean_g = lax.optimization_barrier(jnp.sum(grouped, axis=(0, 2))) / count
    square_g = lax.optimization_barrier(jnp.sum(grouped * grouped, axis=(0, 2))) / count
    inverse = lax.rsqrt(square_g - mean_g * mean_g + 1e-05)
    per_group = C // GROUPS
    return (values - jnp.repeat(mean_g, per_group)) * jnp.repeat(inverse, per_group)

def reference(latent, ada_scale, ada_shift, conv_weight, qkv_weight, out_weight, ancestors):
    head_dim = C // HEADS

    def heads_of(block):
        return block.reshape(H * W, HEADS, head_dim).transpose(1, 0, 2)

    def one_head(triple):
        query_h, key_h, value_h = triple
        scores = jnp.dot(query_h, key_h.T, preferred_element_type=jnp.float32) * head_dim ** (-0.5)
        top = lax.optimization_barrier(jnp.max(scores, axis=1, keepdims=True))
        weights = jnp.exp(scores - top)
        total = lax.optimization_barrier(jnp.sum(weights, axis=1, keepdims=True))
        return jnp.dot(weights.astype(jnp.bfloat16), value_h, preferred_element_type=jnp.float32) / total

    def one_particle(latent_p):
        field = latent_p.astype(jnp.float32).reshape(H * W, C)
        active = jax.nn.silu(group_norm(field) * (1.0 + ada_scale) + ada_shift).astype(jnp.bfloat16)
        padded = jnp.pad(active.reshape(H, W, C), ((1, 1), (1, 1), (0, 0)))
        conv = jnp.zeros((H * W, C), jnp.float32)
        for row_off in range(3):
            for col_off in range(3):
                tap = row_off * 3 + col_off
                window = padded[row_off:row_off + H, col_off:col_off + W].reshape(H * W, C)
                conv = conv + jnp.dot(window, conv_weight[tap * C:(tap + 1) * C], preferred_element_type=jnp.float32)
        resid = lax.optimization_barrier((field + conv).astype(jnp.bfloat16))
        normed = group_norm(resid.astype(jnp.float32)).astype(jnp.bfloat16)
        project = jnp.dot(normed, qkv_weight, preferred_element_type=jnp.float32).astype(jnp.bfloat16)
        triple = (heads_of(project[:, :C]), heads_of(project[:, C:2 * C]), heads_of(project[:, 2 * C:]))
        mixed = lax.map(one_head, triple)
        attended = mixed.transpose(1, 0, 2).reshape(H * W, C).astype(jnp.bfloat16)
        output = resid.astype(jnp.float32) + jnp.dot(attended, out_weight, preferred_element_type=jnp.float32)
        return output.astype(jnp.bfloat16).reshape(H, W, C)
    blocks = lax.map(one_particle, latent)
    return jnp.take(blocks, ancestors.astype(jnp.int32), axis=0)
```

```python
import functools

import jax
import jax.numpy as jnp
from jax import lax
from jax.experimental import pallas as pl
from jax.experimental.pallas import tpu as pltpu
from jax.sharding import PartitionSpec as P

HEADS = 10
GROUPS = 32
INNER = 2
LANES = 128
MESH = pl.DeviceIdType.MESH


def kernel(
    dims,
    anc_ref,
    x_ref,
    scale_ref,
    shift_ref,
    wconv_hbm,
    wqkv_hbm,
    wout_hbm,
    out_ref,
    wconv,
    wqkv,
    wout,
    lat,
    shifted,
    ysend,
    yrecv,
    zsend,
    zrecv,
    own,
    res,
    normed,
    kv,
    att,
    blk,
    blocks,
    load_sem,
    zs1,
    ys1,
    rv1,
    rys,
    ryr,
    rzs,
    rzr,
    zs2,
    ys2,
    rv2,
    ps,
    pr,
):
    rows_here, width, chans, ranks, particles, taps, share = dims
    tokens = rows_here * width
    outer = ranks // INNER
    count = tokens * ranks * (chans // GROUPS)
    head_dim = chans // HEADS
    me = lax.axis_index("rows")
    mine = lax.axis_index("particle")
    a = lax.div(me, INNER)
    b = lax.rem(me, INNER)
    other = a * INNER + (1 - b)

    def ahead(k):
        return lax.rem(a + k, outer)

    def behind(k):
        return lax.rem(a + outer - k, outer)

    loads = [
        pltpu.make_async_copy(wconv_hbm, wconv, load_sem.at[0]),
        pltpu.make_async_copy(wqkv_hbm, wqkv, load_sem.at[1]),
        pltpu.make_async_copy(wout_hbm, wout, load_sem.at[2]),
    ]
    for load in loads:
        load.start()

    barrier = pltpu.get_barrier_semaphore()
    pl.semaphore_signal(barrier, inc=1, device_id={"rows": other}, device_id_type=MESH)
    for k in range(1, outer):
        pl.semaphore_signal(
            barrier, inc=1, device_id={"rows": ahead(k) * INNER + b}, device_id_type=MESH
        )
    for k in range(1, particles):
        pl.semaphore_signal(
            barrier,
            inc=1,
            device_id={"particle": lax.rem(mine + k, particles)},
            device_id_type=MESH,
        )
    pl.semaphore_wait(barrier, outer + particles - 1)

    def to_row(src, dst, send, recv, row):
        return pltpu.make_async_remote_copy(
            src_ref=src,
            dst_ref=dst,
            send_sem=send,
            recv_sem=recv,
            device_id={"rows": row},
            device_id_type=MESH,
        )

    def gather(src, buf, zs, ys, rv):
        total = jnp.zeros((1, chans), jnp.float32)
        square = jnp.zeros((1, chans), jnp.float32)

        def add(v, total, square):
            return (
                total + jnp.sum(v, axis=0, keepdims=True),
                square + jnp.sum(v * v, axis=0, keepdims=True),
            )

        sends = []
        for k in range(outer - 1, 0, -1):
            sends.append(
                to_row(src, buf.at[me], zs.at[k - 1], rv.at[me], ahead(k) * INNER + b)
            )
            sends[-1].start()
        sends.append(to_row(src, buf.at[me], ys.at[0], rv.at[me], other))
        sends[-1].start()
        held = src[...]
        buf[me] = held
        total, square = add(held.astype(jnp.float32), total, square)
        for k in range(1, outer):
            slot = behind(k) * INNER + b
            forward = to_row(buf.at[slot], buf.at[slot], ys.at[k], rv.at[slot], other)
            forward.wait_recv()
            forward.start()
            sends.append(forward)
            total, square = add(buf[slot].astype(jnp.float32), total, square)
        for k in range(outer):
            slot = behind(k) * INNER + (1 - b)
            to_row(buf.at[slot], buf.at[slot], ys.at[k], rv.at[slot], other).wait_recv()
            total, square = add(buf[slot].astype(jnp.float32), total, square)
        return total, square, sends

    per_group = chans // GROUPS
    chan_r = lax.broadcasted_iota(jnp.int32, (chans, LANES), 0)
    group_r = lax.broadcasted_iota(jnp.int32, (chans, LANES), 1) * per_group
    inside = (chan_r >= group_r) & (chan_r < group_r + per_group)
    to_group = jnp.where(inside, 1.0, 0.0).astype(jnp.float32)
    group_c = lax.broadcasted_iota(jnp.int32, (LANES, chans), 0) * per_group
    chan_c = lax.broadcasted_iota(jnp.int32, (LANES, chans), 1)
    inside = (chan_c >= group_c) & (chan_c < group_c + per_group)
    to_chan = jnp.where(inside, 1.0, 0.0).astype(jnp.float32)

    def finish(total, square):
        stacked = jnp.concatenate(
            [total, square, jnp.zeros((6, chans), jnp.float32)], axis=0
        )
        by_group = (
            jnp.dot(
                stacked,
                to_group,
                precision=lax.Precision.HIGHEST,
                preferred_element_type=jnp.float32,
            )
            / count
        )
        mean_g = by_group[0:1]
        inverse = lax.rsqrt(by_group[1:2] - mean_g * mean_g + 1e-05)
        back = jnp.concatenate(
            [mean_g, inverse, jnp.zeros((6, LANES), jnp.float32)], axis=0
        )
        spread = jnp.dot(
            back,
            to_chan,
            precision=lax.Precision.HIGHEST,
            preferred_element_type=jnp.float32,
        )
        return spread[0:1], spread[1:2]

    total, square, sends = gather(x_ref, lat, zs1, ys1, rv1)
    mean_c, inverse_c = finish(total, square)
    gain = 1.0 + scale_ref[...]
    bias = shift_ref[...]
    first = lax.div(me * share, chans)
    tap_ids = [jnp.minimum(first + j, 8) for j in range(taps)]
    column = lax.broadcasted_iota(
        jnp.int32, (rows_here, width, chans), 1
    ).reshape(tokens, chans)
    edge = jnp.zeros((1, width, chans), jnp.float32)
    for j in range(taps):
        shifted[j, 0:1] = edge
        shifted[j, ranks * rows_here + 1 : ranks * rows_here + 2] = edge

    def activate(s, carry):
        v = lat[s].astype(jnp.float32)
        v = (v - mean_c) * inverse_c * gain + bias
        v = (v / (1.0 + jnp.exp(-v))).astype(jnp.bfloat16).astype(jnp.float32)
        left = jnp.where(column == 0, 0.0, pltpu.roll(v, 1, 0))
        right = jnp.where(column == width - 1, 0.0, pltpu.roll(v, tokens - 1, 0))
        for j in range(taps):
            off = lax.rem(tap_ids[j], 3)
            w = jnp.where(off == 0, left, jnp.where(off == 2, right, v))
            shifted[j, pl.ds(1 + s * rows_here, rows_here)] = w.reshape(
                rows_here, width, chans
            )
        return carry

    lax.fori_loop(0, ranks, activate, 0)
    loads[0].wait()

    def conv(slot):
        acc = None
        for j in range(taps):
            window = shifted[j, pl.ds(slot * rows_here + lax.div(tap_ids[j], 3), rows_here)]
            part = jnp.dot(
                window.reshape(tokens, chans).astype(jnp.bfloat16),
                wconv[j * chans : (j + 1) * chans],
                preferred_element_type=jnp.float32,
            )
            acc = part if acc is None else acc + part
        return acc

    order = list(range(1, outer)) + [0]
    for i, k in enumerate(order):
        ysend[i] = conv(ahead(k) * INNER + (1 - b)).astype(jnp.bfloat16)
        sends.append(to_row(ysend.at[i], yrecv.at[i], rys.at[i], ryr.at[i], other))
        sends[-1].start()
    for i, k in enumerate(order):
        part = conv(ahead(k) * INNER + b)
        to_row(ysend.at[i], yrecv.at[i], rys.at[i], ryr.at[i], other).wait_recv()
        part = part + yrecv[i].astype(jnp.float32)
        if k > 0:
            zsend[i] = part.astype(jnp.bfloat16)
            sends.append(
                to_row(
                    zsend.at[i], zrecv.at[i], rzs.at[i], rzr.at[i], ahead(k) * INNER + b
                )
            )
            sends[-1].start()
    for i in range(outer - 1):
        to_row(zsend.at[i], zrecv.at[i], rzs.at[i], rzr.at[i], me).wait_recv()
        part = part + zrecv[i].astype(jnp.float32)
    own[...] = (x_ref[...].astype(jnp.float32) + part).astype(jnp.bfloat16)

    total, square, more = gather(own, res, zs2, ys2, rv2)
    sends += more
    mean_m, inverse_m = finish(total, square)

    def normalize(s, carry):
        v = (res[s].astype(jnp.float32) - mean_m) * inverse_m
        normed[pl.ds(pl.multiple_of(s * tokens, tokens), tokens)] = v.astype(jnp.bfloat16)
        return carry

    lax.fori_loop(0, ranks, normalize, 0)
    loads[1].wait()
    mine_n = ((own[...].astype(jnp.float32) - mean_m) * inverse_m).astype(jnp.bfloat16)
    query = jnp.dot(
        mine_n, wqkv[:, :chans], preferred_element_type=jnp.float32
    ).astype(jnp.bfloat16)
    step = 2 * LANES
    for n in range(2 * chans // step):
        kv[:, n * step : (n + 1) * step] = jnp.dot(
            normed[...],
            wqkv[:, chans + n * step : chans + (n + 1) * step],
            preferred_element_type=jnp.float32,
        ).astype(jnp.bfloat16)

    pair = 2 * head_dim
    lane = lax.broadcasted_iota(jnp.int32, (tokens, pair), 1)
    low = lane < head_dim
    zero = jnp.zeros((tokens, pair), jnp.bfloat16)
    for h in range(HEADS // 2):
        q = query[:, h * pair : (h + 1) * pair]
        q = jnp.concatenate([jnp.where(low, q, zero), jnp.where(low, zero, q)], axis=0)
        scores = lax.dot_general(
            q,
            kv[:, h * pair : (h + 1) * pair],
            (((1,), (1,)), ((), ())),
            preferred_element_type=jnp.float32,
        ) * (head_dim ** (-0.5))
        top = jnp.max(scores, axis=1, keepdims=True)
        weights = jnp.exp(scores - top)
        norm = jnp.sum(weights, axis=1, keepdims=True)
        mixed = (
            jnp.dot(
                weights.astype(jnp.bfloat16),
                kv[:, chans + h * pair : chans + (h + 1) * pair],
                preferred_element_type=jnp.float32,
            )
            / norm
        )
        att[:, h * pair : (h + 1) * pair] = jnp.where(
            low, mixed[:tokens], mixed[tokens:]
        ).astype(jnp.bfloat16)
    loads[2].wait()
    block = (
        own[...].astype(jnp.float32)
        + jnp.dot(att[...], wout[...], preferred_element_type=jnp.float32)
    ).astype(jnp.bfloat16)
    blk[...] = block
    blocks[mine] = block

    def to_particle(k):
        peer = lax.rem(mine + k, particles)
        return pltpu.make_async_remote_copy(
            src_ref=blk,
            dst_ref=blocks.at[mine],
            send_sem=ps.at[k - 1],
            recv_sem=pr.at[k - 1],
            device_id={"particle": peer},
            device_id_type=MESH,
        )

    for k in range(1, particles):
        sends.append(to_particle(k))
        sends[-1].start()
    for k in range(1, particles):
        to_particle(k).wait_recv()
    out_ref[...] = blocks[anc_ref[mine]]
    for send in sends:
        send.wait_send()


def per_device(latent, ada_scale, ada_shift, conv_weight, qkv_weight, out_weight, ancestors):
    _, rows_here, width, chans = latent.shape
    tokens = rows_here * width
    ranks = lax.axis_size("rows")
    particles = lax.axis_size("particle")
    outer = ranks // INNER
    share = conv_weight.shape[0]
    taps = max(-(-((r * share) % chans + share) // chans) for r in range(ranks))
    me = lax.axis_index("rows")
    start = lax.rem(me * share, chans)
    wpad = lax.dynamic_update_slice(
        jnp.zeros((taps * chans, chans), conv_weight.dtype), conv_weight, (start, 0)
    )
    dims = (rows_here, width, chans, ranks, particles, taps, share)
    bf16, f32 = jnp.bfloat16, jnp.float32
    dma = pltpu.SemaphoreType.DMA
    out = pl.pallas_call(
        functools.partial(kernel, dims),
        out_shape=jax.ShapeDtypeStruct((tokens, chans), bf16),
        in_specs=[pl.BlockSpec(memory_space=pltpu.SMEM)]
        + [pl.BlockSpec(memory_space=pltpu.VMEM)] * 3
        + [pl.BlockSpec(memory_space=pl.ANY)] * 3,
        out_specs=pl.BlockSpec(memory_space=pltpu.VMEM),
        scratch_shapes=[
            pltpu.VMEM((taps * chans, chans), bf16),
            pltpu.VMEM(qkv_weight.shape, bf16),
            pltpu.VMEM(out_weight.shape, bf16),
            pltpu.VMEM((ranks, tokens, chans), bf16),
            pltpu.VMEM((taps, ranks * rows_here + 2, width, chans), f32),
            pltpu.VMEM((outer, tokens, chans), bf16),
            pltpu.VMEM((outer, tokens, chans), bf16),
            pltpu.VMEM((outer, tokens, chans), bf16),
            pltpu.VMEM((outer, tokens, chans), bf16),
            pltpu.VMEM((tokens, chans), bf16),
            pltpu.VMEM((ranks, tokens, chans), bf16),
            pltpu.VMEM((ranks * tokens, chans), bf16),
            pltpu.VMEM((ranks * tokens, 2 * chans), bf16),
            pltpu.VMEM((tokens, chans), bf16),
            pltpu.VMEM((tokens, chans), bf16),
            pltpu.VMEM((particles, tokens, chans), bf16),
            dma((3,)),
            dma((outer,)),
            dma((outer,)),
            dma((ranks,)),
            dma((outer,)),
            dma((outer,)),
            dma((outer,)),
            dma((outer,)),
            dma((outer,)),
            dma((outer,)),
            dma((ranks,)),
            dma((particles,)),
            dma((particles,)),
        ],
        compiler_params=pltpu.CompilerParams(
            collective_id=0, has_side_effects=True, vmem_limit_bytes=60000 * 1024
        ),
        name="block",
    )(
        ancestors,
        latent.reshape(tokens, chans),
        ada_scale.reshape(1, chans),
        ada_shift.reshape(1, chans),
        wpad,
        qkv_weight,
        out_weight,
    )
    return out.reshape(latent.shape)


def solution(mesh):
    in_specs = (P("particle", "rows", None, None), P(), P(), P("rows", None), P(), P(), P())
    out_specs = P("particle", "rows", None, None)
    return jax.shard_map(
        per_device, mesh=mesh, in_specs=in_specs, out_specs=out_specs, check_vma=False
    )
```

```python
import functools
import math

import jax
import jax.numpy as jnp
from jax import lax
from jax.experimental import pallas as pl
from jax.experimental.pallas import tpu as pltpu
from jax.sharding import PartitionSpec as P

HEADS = 10
GROUPS = 32
INNER = 2
LANES = 128
MESH = pl.DeviceIdType.MESH


def kernel(
    dims,
    anc_ref,
    x_ref,
    scale_ref,
    shift_ref,
    wconv_hbm,
    wqkv_hbm,
    wout_hbm,
    out_ref,
    wconv,
    wqkv,
    wout,
    lat,
    shifted,
    ysend,
    yrecv,
    zsend,
    zrecv,
    own,
    res,
    normed,
    kv,
    att,
    blk,
    blocks,
    stat,
    load_sem,
    up1,
    down1,
    ys1,
    rv1,
    rys,
    ryr,
    rzs,
    rzr,
    up2,
    down2,
    ys2,
    rv2,
    ps,
    pr,
):
    rows_here, width, chans, ranks, particles, taps, share = dims
    tokens = rows_here * width
    outer = ranks // INNER
    count = tokens * ranks * (chans // GROUPS)
    head_dim = chans // HEADS
    me = lax.axis_index("rows")
    mine = lax.axis_index("particle")
    a = lax.div(me, INNER)
    b = lax.rem(me, INNER)
    other = a * INNER + (1 - b)

    def ahead(k):
        return lax.rem(a + k, outer)

    def behind(k):
        return lax.rem(a + outer - k, outer)

    padded = wconv_hbm.shape[0] == wconv.shape[0]
    if padded:
        weights_in = wconv
    else:
        grain = math.gcd(share, chans)
        skip = lax.rem(me * (share // grain), chans // grain)
        weights_in = wconv.at[pl.ds(pl.multiple_of(skip * grain, grain), share)]
    loads = [
        pltpu.make_async_copy(wconv_hbm, weights_in, load_sem.at[0]),
        pltpu.make_async_copy(wqkv_hbm, wqkv, load_sem.at[1]),
        pltpu.make_async_copy(wout_hbm, wout, load_sem.at[2]),
    ]
    for load in loads:
        load.start()

    if not padded:
        for i in range(taps * chans // grain):

            @pl.when((skip > i) | (skip + share // grain <= i))
            def _():
                wconv[i * grain : (i + 1) * grain] = jnp.zeros((grain, chans), wconv.dtype)

    barrier = pltpu.get_barrier_semaphore()
    pl.semaphore_signal(barrier, inc=1, device_id={"rows": other}, device_id_type=MESH)
    for k in range(1, outer):
        pl.semaphore_signal(
            barrier, inc=1, device_id={"rows": ahead(k) * INNER + b}, device_id_type=MESH
        )
    for k in range(1, particles):
        pl.semaphore_signal(
            barrier,
            inc=1,
            device_id={"particle": lax.rem(mine + k, particles)},
            device_id_type=MESH,
        )
    pl.semaphore_wait(barrier, outer + particles - 1)

    def to_row(src, dst, send, recv, row):
        return pltpu.make_async_remote_copy(
            src_ref=src,
            dst_ref=dst,
            send_sem=send,
            recv_sem=recv,
            device_id={"rows": row},
            device_id_type=MESH,
        )

    half = tokens // 2

    def part_of(buf, slot, piece):
        return buf.at[slot, pl.ds(piece * half, half)]

    def gather(src, buf, up, down, across, rv):
        stat[...] = jnp.zeros_like(stat)

        def add(slot):
            v = buf[slot].astype(jnp.float32)
            stat[0:1] += jnp.sum(v, axis=0, keepdims=True)
            stat[1:2] += jnp.sum(v * v, axis=0, keepdims=True)

        def copy(slot, piece, sems, row, mine_too=False):
            here = src.at[pl.ds(piece * half, half)] if mine_too else part_of(buf, slot, piece)
            return to_row(
                here, part_of(buf, slot, piece), sems.at[slot, piece], rv.at[slot, piece], row
            )

        def both(slot, piece, act, own_too=False):
            @pl.when(a + 1 < outer)
            def _():
                act(copy(slot, piece, up, (a + 1) * INNER + b, own_too))

            @pl.when(a > 0)
            def _():
                act(copy(slot, piece, down, (a - 1) * INNER + b, own_too))

        def start(c):
            c.start()

        def done(c):
            c.wait_send()

        def arrived(slot, piece):
            copy(slot, piece, across, other).wait_recv()

        copy(me, 1, across, other, True).start()
        both(me, 0, start, True)
        both(me, 1, start, True)
        copy(me, 0, across, other, True).start()
        buf[me] = src[...]
        add(me)
        arrived(other, 1)
        both(other, 1, start)
        for t in range(1, outer):
            sides = (
                (a >= t, a - t, a + 1 < outer, up, a + 1),
                (a + t < outer, a + t, a > 0, down, a - 1),
            )
            for present, origin, onward, sems, target in sides:
                near = origin * INNER + b
                far = origin * INNER + (1 - b)
                row = target * INNER + b
                for slot, piece in ((near, 0), (near, 1), (far, 1)):

                    @pl.when(present)
                    def _():
                        arrived(slot, piece)

                    @pl.when(present & onward)
                    def _():
                        copy(slot, piece, sems, row).start()

                    if piece == 0:

                        @pl.when(present)
                        def _():
                            copy(slot, piece, across, other).start()

                @pl.when(present)
                def _():
                    add(near)

        arrived(other, 0)
        add(other)
        for t in range(1, outer):
            for present, origin in ((a >= t, a - t), (a + t < outer, a + t)):

                @pl.when(present)
                def _():
                    slot = origin * INNER + (1 - b)
                    arrived(slot, 0)
                    add(slot)

        def finish_sends():
            copy(me, 1, across, other, True).wait_send()
            copy(me, 0, across, other, True).wait_send()
            both(me, 0, done, True)
            both(me, 1, done, True)
            both(other, 1, done)
            for t in range(1, outer):
                sides = (
                    (a >= t, a - t, a + 1 < outer, up, a + 1),
                    (a + t < outer, a + t, a > 0, down, a - 1),
                )
                for present, origin, onward, sems, target in sides:
                    near = origin * INNER + b
                    far = origin * INNER + (1 - b)
                    row = target * INNER + b

                    @pl.when(present & onward)
                    def _():
                        for slot, piece in ((near, 0), (near, 1), (far, 1)):
                            copy(slot, piece, sems, row).wait_send()

                    @pl.when(present)
                    def _():
                        copy(near, 0, across, other).wait_send()

        return stat[0:1], stat[1:2], finish_sends

    per_group = chans // GROUPS
    chan_r = lax.broadcasted_iota(jnp.int32, (chans, LANES), 0)
    group_r = lax.broadcasted_iota(jnp.int32, (chans, LANES), 1) * per_group
    inside = (chan_r >= group_r) & (chan_r < group_r + per_group)
    to_group = jnp.where(inside, 1.0, 0.0).astype(jnp.float32)
    group_c = lax.broadcasted_iota(jnp.int32, (LANES, chans), 0) * per_group
    chan_c = lax.broadcasted_iota(jnp.int32, (LANES, chans), 1)
    inside = (chan_c >= group_c) & (chan_c < group_c + per_group)
    to_chan = jnp.where(inside, 1.0, 0.0).astype(jnp.float32)

    def finish(total, square):
        stacked = jnp.concatenate(
            [total, square, jnp.zeros((6, chans), jnp.float32)], axis=0
        )
        by_group = (
            jnp.dot(
                stacked,
                to_group,
                precision=lax.Precision.HIGHEST,
                preferred_element_type=jnp.float32,
            )
            / count
        )
        mean_g = by_group[0:1]
        inverse = lax.rsqrt(by_group[1:2] - mean_g * mean_g + 1e-05)
        back = jnp.concatenate(
            [mean_g, inverse, jnp.zeros((6, LANES), jnp.float32)], axis=0
        )
        spread = jnp.dot(
            back,
            to_chan,
            precision=lax.Precision.HIGHEST,
            preferred_element_type=jnp.float32,
        )
        return spread[0:1], spread[1:2]

    total, square, finish_first = gather(x_ref, lat, up1, down1, ys1, rv1)
    sends = []
    mean_c, inverse_c = finish(total, square)
    gain = 1.0 + scale_ref[...].reshape(1, chans)
    bias = shift_ref[...].reshape(1, chans)
    first = lax.div(me * share, chans)
    tap_ids = [jnp.minimum(first + j, 8) for j in range(taps)]
    column = lax.broadcasted_iota(
        jnp.int32, (rows_here, width, chans), 1
    ).reshape(tokens, chans)
    edge = jnp.zeros((1, width, chans), jnp.float32)
    for j in range(taps):
        shifted[j, 0:1] = edge
        shifted[j, ranks * rows_here + 1 : ranks * rows_here + 2] = edge

    def activate(s, carry):
        v = lat[s].astype(jnp.float32)
        v = (v - mean_c) * inverse_c * gain + bias
        v = (v / (1.0 + jnp.exp(-v))).astype(jnp.bfloat16).astype(jnp.float32)
        left = jnp.where(column == 0, 0.0, pltpu.roll(v, 1, 0))
        right = jnp.where(column == width - 1, 0.0, pltpu.roll(v, tokens - 1, 0))
        for j in range(taps):
            off = lax.rem(tap_ids[j], 3)
            w = jnp.where(off == 0, left, jnp.where(off == 2, right, v))
            shifted[j, pl.ds(1 + s * rows_here, rows_here)] = w.reshape(
                rows_here, width, chans
            )
        return carry

    lax.fori_loop(0, ranks, activate, 0)
    loads[0].wait()

    def conv(slot):
        acc = None
        for j in range(taps):
            window = shifted[j, pl.ds(slot * rows_here + lax.div(tap_ids[j], 3), rows_here)]
            part = jnp.dot(
                window.reshape(tokens, chans).astype(jnp.bfloat16),
                wconv[j * chans : (j + 1) * chans],
                preferred_element_type=jnp.float32,
            )
            acc = part if acc is None else acc + part
        return acc

    order = list(range(1, outer)) + [0]
    for i, k in enumerate(order):
        ysend[i] = conv(ahead(k) * INNER + (1 - b)).astype(jnp.bfloat16)
        sends.append(to_row(ysend.at[i], yrecv.at[i], rys.at[i], ryr.at[i], other))
        sends[-1].start()
    for i, k in enumerate(order):
        part = conv(ahead(k) * INNER + b)
        to_row(ysend.at[i], yrecv.at[i], rys.at[i], ryr.at[i], other).wait_recv()
        part = part + yrecv[i].astype(jnp.float32)
        if k > 0:
            zsend[i] = part.astype(jnp.bfloat16)
            sends.append(
                to_row(
                    zsend.at[i], zrecv.at[i], rzs.at[i], rzr.at[i], ahead(k) * INNER + b
                )
            )
            sends[-1].start()
    for i in range(outer - 1):
        to_row(zsend.at[i], zrecv.at[i], rzs.at[i], rzr.at[i], me).wait_recv()
        part = part + zrecv[i].astype(jnp.float32)
    own[...] = (x_ref[...].astype(jnp.float32) + part).astype(jnp.bfloat16)

    total, square, finish_second = gather(own, res, up2, down2, ys2, rv2)
    mean_m, inverse_m = finish(total, square)

    def normalize(s, carry):
        v = (res[s].astype(jnp.float32) - mean_m) * inverse_m
        normed[pl.ds(pl.multiple_of(s * tokens, tokens), tokens)] = v.astype(jnp.bfloat16)
        return carry

    lax.fori_loop(0, ranks, normalize, 0)
    loads[1].wait()
    mine_n = ((own[...].astype(jnp.float32) - mean_m) * inverse_m).astype(jnp.bfloat16)
    query = jnp.dot(
        mine_n, wqkv[:, :chans], preferred_element_type=jnp.float32
    ).astype(jnp.bfloat16)
    step = 2 * LANES
    for n in range(2 * chans // step):
        kv[:, n * step : (n + 1) * step] = jnp.dot(
            normed[...],
            wqkv[:, chans + n * step : chans + (n + 1) * step],
            preferred_element_type=jnp.float32,
        ).astype(jnp.bfloat16)

    pair = 2 * head_dim
    lane = lax.broadcasted_iota(jnp.int32, (tokens, pair), 1)
    low = lane < head_dim
    zero = jnp.zeros((tokens, pair), jnp.bfloat16)
    for h in range(HEADS // 2):
        q = query[:, h * pair : (h + 1) * pair]
        q = jnp.concatenate([jnp.where(low, q, zero), jnp.where(low, zero, q)], axis=0)
        scores = lax.dot_general(
            q,
            kv[:, h * pair : (h + 1) * pair],
            (((1,), (1,)), ((), ())),
            preferred_element_type=jnp.float32,
        ) * (head_dim ** (-0.5))
        top = jnp.max(scores, axis=1, keepdims=True)
        weights = jnp.exp(scores - top)
        norm = jnp.sum(weights, axis=1, keepdims=True)
        mixed = (
            jnp.dot(
                weights.astype(jnp.bfloat16),
                kv[:, chans + h * pair : chans + (h + 1) * pair],
                preferred_element_type=jnp.float32,
            )
            / norm
        )
        att[:, h * pair : (h + 1) * pair] = jnp.where(
            low, mixed[:tokens], mixed[tokens:]
        ).astype(jnp.bfloat16)
    loads[2].wait()
    block = (
        own[...].astype(jnp.float32)
        + jnp.dot(att[...], wout[...], preferred_element_type=jnp.float32)
    ).astype(jnp.bfloat16)
    blk[...] = block
    blocks[mine] = block

    def to_particle(k):
        peer = lax.rem(mine + k, particles)
        return pltpu.make_async_remote_copy(
            src_ref=blk,
            dst_ref=blocks.at[mine],
            send_sem=ps.at[k - 1],
            recv_sem=pr.at[k - 1],
            device_id={"particle": peer},
            device_id_type=MESH,
        )

    for k in range(1, particles):
        sends.append(to_particle(k))
        sends[-1].start()
    for k in range(1, particles):
        to_particle(k).wait_recv()
    out_ref[...] = blocks[anc_ref[mine]]
    for send in sends:
        send.wait_send()
    finish_first()
    finish_second()


def per_device(latent, ada_scale, ada_shift, conv_weight, qkv_weight, out_weight, ancestors):
    _, rows_here, width, chans = latent.shape
    tokens = rows_here * width
    ranks = lax.axis_size("rows")
    particles = lax.axis_size("particle")
    outer = ranks // INNER
    share = conv_weight.shape[0]
    taps = max(-(-((r * share) % chans + share) // chans) for r in range(ranks))
    wpad = conv_weight
    if math.gcd(share, chans) % 16:
        start = lax.rem(lax.axis_index("rows") * share, chans)
        wpad = lax.dynamic_update_slice(
            jnp.zeros((taps * chans, chans), wpad.dtype), wpad, (start, 0)
        )
    dims = (rows_here, width, chans, ranks, particles, taps, share)
    bf16, f32 = jnp.bfloat16, jnp.float32
    dma = pltpu.SemaphoreType.DMA
    out = pl.pallas_call(
        functools.partial(kernel, dims),
        out_shape=jax.ShapeDtypeStruct((tokens, chans), bf16),
        in_specs=[pl.BlockSpec(memory_space=pltpu.SMEM)]
        + [pl.BlockSpec(memory_space=pltpu.VMEM)] * 3
        + [pl.BlockSpec(memory_space=pl.ANY)] * 3,
        out_specs=pl.BlockSpec(memory_space=pltpu.VMEM),
        scratch_shapes=[
            pltpu.VMEM((taps * chans, chans), bf16),
            pltpu.VMEM(qkv_weight.shape, bf16),
            pltpu.VMEM(out_weight.shape, bf16),
            pltpu.VMEM((ranks, tokens, chans), bf16),
            pltpu.VMEM((taps, ranks * rows_here + 2, width, chans), f32),
            pltpu.VMEM((outer, tokens, chans), bf16),
            pltpu.VMEM((outer, tokens, chans), bf16),
            pltpu.VMEM((outer, tokens, chans), bf16),
            pltpu.VMEM((outer, tokens, chans), bf16),
            pltpu.VMEM((tokens, chans), bf16),
            pltpu.VMEM((ranks, tokens, chans), bf16),
            pltpu.VMEM((ranks * tokens, chans), bf16),
            pltpu.VMEM((ranks * tokens, 2 * chans), bf16),
            pltpu.VMEM((tokens, chans), bf16),
            pltpu.VMEM((tokens, chans), bf16),
            pltpu.VMEM((particles, tokens, chans), bf16),
            pltpu.VMEM((8, chans), f32),
            dma((3,)),
            dma((ranks, 2)),
            dma((ranks, 2)),
            dma((ranks, 2)),
            dma((ranks, 2)),
            dma((outer,)),
            dma((outer,)),
            dma((outer,)),
            dma((outer,)),
            dma((ranks, 2)),
            dma((ranks, 2)),
            dma((ranks, 2)),
            dma((ranks, 2)),
            dma((particles,)),
            dma((particles,)),
        ],
        compiler_params=pltpu.CompilerParams(
            collective_id=0, has_side_effects=True, vmem_limit_bytes=60000 * 1024
        ),
        name="block",
    )(
        ancestors,
        latent.reshape(tokens, chans),
        ada_scale,
        ada_shift,
        wpad,
        qkv_weight,
        out_weight,
    )
    return out.reshape(latent.shape)


def solution(mesh):
    in_specs = (P("particle", "rows", None, None), P(), P(), P("rows", None), P(), P(), P())
    out_specs = P("particle", "rows", None, None)
    return jax.shard_map(
        per_device, mesh=mesh, in_specs=in_specs, out_specs=out_specs, check_vma=False
    )
```
